32 devices in a mesh: wide: 8 (over z, x), tensor: 4 (over y, core).
Axes of the slice: x: 2, y: 2, z: 4, core: 2. Of those that a mesh axis runs over, the one named last changes fastest.
Arguments:
- tokens: bfloat16 [2, 12544, 768], P(None, ('wide', 'tensor')), may hold values from -6 to 6
- cotangent: bfloat16 [2, 12544, 768], P(None, ('wide', 'tensor')), may hold values from -6 to 6
- ln_gain: bfloat16 [3, 768], P(None, 'wide'), may hold values from 0.25 to 1.75
- biases: bfloat16 [10, 768], P(None, 'wide'), may hold values from -1.1953125 to 1.1953125
- fc1_bias: bfloat16 [3072], P('wide'), may hold values from -1.1953125 to 1.1953125
- w_qkv_s: bfloat16 [3, 768, 768], P(None, 'wide', 'tensor'), may hold values from -0.21875 to 0.21875
- w_out_s: bfloat16 [768, 768], P('tensor', 'wide'), may hold values from -2.5 to 2.5
- w_qkv_t: bfloat16 [3, 768, 768], P(None, 'wide', 'tensor'), may hold values from -0.21875 to 0.21875
- w_out_t: bfloat16 [768, 768], P('tensor', 'wide'), may hold values from -0.625 to 0.625
- w_up: bfloat16 [768, 3072], P('wide', 'tensor'), may hold values from -0.21875 to 0.21875
- w_down: bfloat16 [3072, 768], P('tensor', 'wide'), may hold values from -0.109375 to 0.109375
Outputs:
- mixed: bfloat16 [2, 12544, 768], P(None, ('wide', 'tensor'))
- grad_tokens: float32 [2, 12544, 768], P(None, ('wide', 'tensor'))
- grad_ln_gain: float32 [3, 768], P(None, 'wide')
- grad_biases: float32 [10, 768], P(None, 'wide')
- grad_fc1_bias: float32 [3072], P('wide')
- grad_w_qkv_s: float32 [3, 768, 768], P(None, 'wide', 'tensor')
- grad_w_out_s: float32 [768, 768], P('tensor', 'wide')
- grad_w_qkv_t: float32 [3, 768, 768], P(None, 'wide', 'tensor')
- grad_w_out_t: float32 [768, 768], P('tensor', 'wide')
- grad_w_up: float32 [768, 3072], P('wide', 'tensor')
- grad_w_down: float32 [3072, 768], P('tensor', 'wide')
The draws below stay inside these ranges and needn't reach their ends.
All inputs are finite; a program needn't handle non-finite values.
Results may differ from the reference program's by a relative error of at most 0.014.
Values may be sent and summed in bfloat16 or wider, within the bound.
No kernel may reach another device: no remote copies, remote signals or barrier semaphores. Data moves between devices by JAX's collectives and lax.ppermute only.
A program may use at most 256 MiB of HBM per device.

```python
import jax
import jax.numpy as jnp
from jax import lax

D = 768
HEADS = 12
HEAD_DIM = 64
FF = 3072
PATCHES = 196
FRAMES = 16
FRAME_RUN = 2
MB = 2
CLIPS = 4
TOKENS = 12544


def levels(key, extent, cuts, low, largest):
    level, own = 1.0, jax.random.fold_in(key, 6)
    for axis_at, parts in cuts:
        draws = jnp.exp(jax.random.uniform(jax.random.fold_in(own, axis_at), (parts,), jnp.float32, low / len(cuts), largest / len(cuts)))
        level = level * jnp.repeat(draws, extent[axis_at] // parts).reshape([-1 if axis == axis_at else 1 for axis in range(len(extent))])
    return level


def normal_values(own_key, shape, scale, reach, split=(), dtype=jnp.bfloat16):
    array = jax.random.normal(own_key, shape, jnp.float32) * scale
    if len(split) > 0:
        array = levels(own_key, shape, split, -0.22, 0.18) * array
    return jnp.clip(array, min=-reach, max=reach).astype(dtype)


def setup_inputs(seed: int = 0) -> dict:
    splits = jax.random.split(jax.random.key(seed), 12)
    tokens = normal_values(splits[0], (MB, TOKENS, D), 1.0, 6.0, ((1, 32),))
    cotangent = normal_values(splits[1], (MB, TOKENS, D), 1.0, 6.0, ((1, 32),))
    ln_gain = jnp.clip(1.0 + 0.15 * jax.random.normal(splits[2], (3, D), jnp.float32), 0.25, 1.75).astype(jnp.bfloat16)
    biases = normal_values(splits[3], (10, D), 0.2, 1.1953125, ((1, 8),))
    fc1_bias = normal_values(splits[4], (FF,), 0.2, 1.1953125, ((0, 8),))
    w_qkv_s = normal_values(splits[5], (3, D, D), D ** -0.5, 0.21875, ((1, 8), (2, 4)))
    w_out_s = normal_values(splits[6], (D, D), (max(D // PATCHES * 2, 1)) ** -0.5, 2.5, ((0, 4), (1, 8)))
    w_qkv_t = normal_values(splits[7], (3, D, D), D ** -0.5, 0.21875, ((1, 8), (2, 4)))
    w_out_t = normal_values(splits[8], (D, D), (max(D // FRAMES * 2, 1)) ** -0.5, 0.625, ((0, 4), (1, 8)))
    w_up = normal_values(splits[9], (D, FF), D ** -0.5, 0.21875, ((0, 8), (1, 4)))
    w_down = normal_values(splits[10], (FF, D), FF ** -0.5, 0.109375, ((0, 4), (1, 8)))
    return {"tokens": tokens, "cotangent": cotangent, "ln_gain": ln_gain, "biases": biases, "fc1_bias": fc1_bias, "w_qkv_s": w_qkv_s, "w_out_s": w_out_s, "w_qkv_t": w_qkv_t, "w_out_t": w_out_t, "w_up": w_up, "w_down": w_down}


@jax.custom_vjp
def low(v):
    return lax.optimization_barrier(v.astype(jnp.bfloat16)).astype(jnp.float32)

@jax.custom_vjp
def low_back(v):
    return v

def low_keep(v):
    return (low(v), None)

def low_pass(kept, grad):
    return (grad,)

def back_keep(v):
    return (v, None)

def back_low(kept, grad):
    return (low(grad),)
low.defvjp(low_keep, low_pass)
low_back.defvjp(back_keep, back_low)
EPSILON = 1e-06
HIGHEST = lax.Precision.HIGHEST

def layer_norm(rows, gain, shift):
    center = rows - lax.optimization_barrier(jnp.mean(rows, axis=-1, keepdims=True))
    spread = lax.optimization_barrier(jnp.mean(center * center, axis=-1, keepdims=True))
    return center * lax.rsqrt(spread + EPSILON) * gain + shift

def attend(normed, w_qkv, bias_query, bias_value, w_out, score_form, out_form):
    queries = low(low_back(jnp.dot(normed, w_qkv[0], precision=HIGHEST) + bias_query))
    key_rows = low(low_back(jnp.dot(normed, w_qkv[1], precision=HIGHEST)))
    value_rows = low(low_back(jnp.dot(normed, w_qkv[2], precision=HIGHEST) + bias_value))
    split_shape = normed.shape[:-1] + (HEADS, HEAD_DIM)
    queries = queries.reshape(split_shape)
    key_rows = key_rows.reshape(split_shape)
    value_rows = value_rows.reshape(split_shape)
    scores = low_back(jnp.einsum(score_form, queries, key_rows, precision=HIGHEST) * HEAD_DIM ** (-0.5))
    weights = low(jax.nn.softmax(scores, axis=-1))
    result = jnp.einsum(out_form, weights, value_rows, precision=HIGHEST)
    result = low(low_back(result.reshape(normed.shape)))
    return low_back(jnp.dot(result, w_out, precision=HIGHEST))

def clip_forward(block, ln_gain, biases, fc1_bias, w_qkv_s, w_out_s, w_qkv_t, w_out_t, w_up, w_down):
    normed = low(layer_norm(block, ln_gain[0], biases[0]))
    block = block + attend(normed, w_qkv_s, biases[3], biases[4], w_out_s, 'fphe,fqhe->fhpq', 'fhpq,fqhe->fphe') + biases[5]
    normed = low(layer_norm(block, ln_gain[1], biases[1]))
    block = block + attend(normed, w_qkv_t, biases[6], biases[7], w_out_t, 'tphe,uphe->phtu', 'phtu,uphe->tphe') + biases[8]
    normed = low(layer_norm(block, ln_gain[2], biases[2]))
    pre_act = low_back(jnp.dot(normed, w_up, precision=HIGHEST) + fc1_bias)
    activ = low(jax.nn.gelu(pre_act, approximate=False))
    return block + low_back(jnp.dot(activ, w_down, precision=HIGHEST)) + biases[9]

def reference(tokens, cotangent, ln_gain, biases, fc1_bias, w_qkv_s, w_out_s, w_qkv_t, w_out_t, w_up, w_down):
    params = tuple((item.astype(jnp.float32) for item in (ln_gain, biases, fc1_bias, w_qkv_s, w_out_s, w_qkv_t, w_out_t, w_up, w_down)))

    def forward(inputs, *weights):
        clip_rows = inputs.reshape(MB, FRAMES // FRAME_RUN, CLIPS, FRAME_RUN, PATCHES, D).transpose(0, 2, 1, 3, 4, 5).reshape(MB * CLIPS, FRAMES, PATCHES, D)
        stepper = jax.checkpoint(lambda block: clip_forward(block, *weights))
        result = lax.map(stepper, clip_rows)
        return result.reshape(MB, CLIPS, FRAMES // FRAME_RUN, FRAME_RUN, PATCHES, D).transpose(0, 2, 1, 3, 4, 5).reshape(inputs.shape)
    mixed, pullback = jax.vjp(forward, tokens.astype(jnp.float32), *params)
    grads = pullback(cotangent.astype(jnp.float32))
    return (mixed.astype(jnp.bfloat16), grads[0], grads[1], grads[2], grads[3], grads[4], grads[5], grads[6], grads[7], grads[8], grads[9])
```

```python
import jax
import jax.numpy as jnp
from jax import lax
from jax.sharding import PartitionSpec as P

HEAD_DIM = 64
PATCHES = 196
FRAMES = 16
FRAME_RUN = 2
EPSILON = 1e-06
RUNS = FRAMES // FRAME_RUN

BF = jnp.bfloat16
F32 = jnp.float32


def swap(block, axis, bits):
    size = lax.axis_size(axis)
    return lax.ppermute(block, axis, [(i, i ^ bits) for i in range(size)])


def dot(left, right, dims):
    return lax.dot_general(left, right, (dims, ((), ())), preferred_element_type=F32)


def gather_wide(shard):
    count = lax.axis_size("wide")
    if count != 8:
        return lax.all_gather(shard, "wide", axis=0, tiled=True)
    pieces = {0: shard, 1: swap(shard, "wide", 1)}
    for bits in (2, 4, 6):
        pieces[bits] = swap(shard, "wide", bits)
    for bits in (2, 4, 6):
        pieces[bits ^ 1] = swap(pieces[bits], "wide", 1)
    rows = shard.shape[0]
    me = lax.axis_index("wide")
    whole = jnp.zeros((count * rows, shard.shape[1]), shard.dtype)
    for bits in range(count):
        whole = lax.dynamic_update_slice(whole, pieces[bits], ((me ^ bits) * rows, 0))
    return whole


def gather_tensor(block):
    far = swap(block, "tensor", 2)
    return [block, swap(block, "tensor", 1), far, swap(far, "tensor", 1)]


def reduce_all(parts):
    near = parts[0].astype(F32) + swap(parts[1].astype(BF), "tensor", 1).astype(F32)
    far = parts[2].astype(F32) + swap(parts[3].astype(BF), "tensor", 1).astype(F32)
    total = near + swap(far.astype(BF), "tensor", 2).astype(F32)
    return reduce_wide(total, BF)


def reduce_wide(total, link):
    count = lax.axis_size("wide")
    if count != 8:
        return lax.psum_scatter(total, "wide", scatter_dimension=0, tiled=True)
    me = lax.axis_index("wide")
    grid = total.reshape(4, 2, total.shape[0] // 8, total.shape[1])
    mine = lax.dynamic_index_in_dim(grid, me & 1, 1, keepdims=False)
    other = lax.dynamic_index_in_dim(grid, 1 - (me & 1), 1, keepdims=False)
    half = mine + swap(other.astype(link), "wide", 1).astype(F32)
    place = me >> 1
    result = lax.dynamic_index_in_dim(half, place, 0, keepdims=False)
    for bits in (1, 2, 3):
        piece = lax.dynamic_index_in_dim(half, place ^ bits, 0, keepdims=False)
        result = result + swap(piece.astype(link), "wide", bits * 2).astype(F32)
    return result


def exchange(block):
    count = lax.axis_size("wide")
    stride = count // RUNS
    groups = [[run * stride + clip for run in range(RUNS)] for clip in range(stride)]
    return lax.all_to_all(
        block, "wide", split_axis=0, concat_axis=0, tiled=True, axis_index_groups=groups
    )


def to_patches(rows, micro):
    width = rows.shape[-1]
    share = micro * PATCHES // RUNS
    cut = PATCHES // share
    block = rows.reshape(micro, FRAME_RUN, cut, share, width).swapaxes(1, 2)
    return exchange(block.reshape(RUNS, FRAME_RUN * share, width)).reshape(-1, width)


def to_frames(rows, micro):
    width = rows.shape[-1]
    share = micro * PATCHES // RUNS
    cut = PATCHES // share
    block = exchange(rows.reshape(RUNS, FRAME_RUN * share, width))
    block = block.reshape(micro, cut, FRAME_RUN, share, width).swapaxes(1, 2)
    return block.reshape(-1, width)


def norm_parts(rows):
    center = rows - jnp.mean(rows, axis=-1, keepdims=True)
    scale = lax.rsqrt(jnp.mean(center * center, axis=-1, keepdims=True) + EPSILON)
    return center * scale, scale


def norm(rows, gain, shift):
    hat, _ = norm_parts(rows)
    return (hat * gain + shift).astype(BF)


def norm_back(rows, gain, grad):
    hat, scale = norm_parts(rows)
    back = grad * gain
    inner = jnp.mean(back * hat, axis=-1, keepdims=True)
    result = scale * (back - jnp.mean(back, axis=-1, keepdims=True) - hat * inner)
    return result, jnp.sum(grad * hat, axis=0), jnp.sum(grad, axis=0)


SPATIAL = ("fphe,fqhe->fhpq", "fhpq,fqhe->fphe", "fhpq,fphe->fqhe")
TEMPORAL = ("tphe,uphe->phtu", "phtu,uphe->tphe", "phtu,tphe->uphe")


def heads_of(joined, shape):
    return joined.reshape(shape + (joined.shape[-1] // HEAD_DIM, HEAD_DIM))


def attend(queries, key_rows, value_rows, forms):
    scores = jnp.einsum(forms[0], queries, key_rows, preferred_element_type=F32)
    weights = jax.nn.softmax(scores * HEAD_DIM**-0.5, axis=-1)
    result = jnp.einsum(forms[1], weights.astype(BF), value_rows, preferred_element_type=F32)
    return weights, result.astype(BF)


def attend_back(queries, key_rows, value_rows, weights, grad_out, forms):
    grad_w = jnp.einsum(forms[0], grad_out, value_rows, preferred_element_type=F32)
    inner = jnp.sum(weights * grad_w, axis=-1, keepdims=True)
    grad_s = (weights * (grad_w - inner)).astype(BF)
    scale = HEAD_DIM**-0.5
    grad_q = jnp.einsum(forms[1], grad_s, key_rows, preferred_element_type=F32) * scale
    grad_k = jnp.einsum(forms[2], grad_s, queries, preferred_element_type=F32) * scale
    grad_v = jnp.einsum(forms[2], weights.astype(BF), grad_out, preferred_element_type=F32)
    return grad_q.astype(BF), grad_k.astype(BF), grad_v.astype(BF)


def branch(rows, packs, biases, cols, shape, forms):
    parts = [dot(rows, pack[:, : 3 * cols], ((1,), (0,))) for pack in packs]
    joined = []
    for which in range(3):
        sides = [part[:, which * cols : (which + 1) * cols] for part in parts]
        whole = jnp.concatenate(sides, axis=1)
        if which != 1:
            whole = whole + biases[which // 2]
        joined.append(heads_of(whole.astype(BF), shape))
    weights, mixed = attend(*joined, forms)
    mixed = mixed.reshape(rows.shape)
    out = sum(
        dot(mixed[:, r * cols : (r + 1) * cols], packs[r][:, 3 * cols :], ((1,), (1,)))
        for r in range(4)
    )
    return joined, weights, mixed, out


def branch_back(rows, packs, kept, grad, cols, shape, forms):
    joined, weights, mixed = kept
    grad_mixed = jnp.concatenate(
        [dot(grad, pack[:, 3 * cols :], ((1,), (0,))) for pack in packs], axis=1
    ).astype(BF)
    grads = attend_back(*joined, weights, heads_of(grad_mixed, shape), forms)
    grads = [item.reshape(rows.shape) for item in grads]
    sums, grad_rows = [], 0.0
    for r in range(4):
        span = slice(r * cols, (r + 1) * cols)
        side = jnp.concatenate([item[:, span] for item in grads], axis=1)
        grad_rows = grad_rows + dot(side, packs[r][:, : 3 * cols], ((1,), (1,)))
        first = dot(rows, side, ((0,), (0,)))
        second = dot(grad, mixed[:, span], ((0,), (0,)))
        sums.append(jnp.concatenate([first, second], axis=1).astype(BF))
    bias_sums = [jnp.sum(grads[i].astype(F32), axis=0) for i in (0, 2)]
    return grad_rows, sums, bias_sums


def per_device(
    tokens, cotangent, ln_gain, biases, fc1_bias, w_qkv_s, w_out_s, w_qkv_t, w_out_t, w_up, w_down
):
    micro, row_count, width = tokens.shape
    wide_count = lax.axis_size("wide")
    tensor_count = lax.axis_size("tensor")
    me_t = lax.axis_index("tensor")
    cols = w_qkv_s.shape[2]
    hidden = w_up.shape[1]
    slim = ln_gain.shape[1]
    assert row_count == FRAME_RUN * PATCHES and tensor_count == 4
    assert wide_count % RUNS == 0 and (micro * PATCHES) % RUNS == 0

    def pack(w_qkv, w_out):
        return jnp.concatenate([w_qkv[0], w_qkv[1], w_qkv[2], w_out.T], axis=1)

    shards = [pack(w_qkv_s, w_out_s), pack(w_qkv_t, w_out_t), w_up, w_down.T]
    small = jnp.concatenate([ln_gain, biases, fc1_bias.reshape(-1, slim)], axis=0)
    extra = small.shape[0]
    small = lax.all_gather(small, "wide", axis=0).astype(F32)
    vectors = small[:, :13].swapaxes(0, 1).reshape(13, width)
    gains, shifts = vectors[:3], vectors[3:]
    fc1 = small[:, 13:].reshape(-1)
    order = [me_t ^ r for r in range(4)]

    def turned(vector, size):
        return jnp.concatenate(
            [lax.dynamic_slice_in_dim(vector, index * size, size) for index in order]
        )

    pack_s, pack_t, pack_u, pack_d = [gather_tensor(gather_wide(shard)) for shard in shards]

    source = tokens.reshape(micro * row_count, width).astype(F32)
    frame_shape = (micro * FRAME_RUN, PATCHES)
    clip_shape = (FRAMES, micro * PATCHES // RUNS)
    grad_out = to_patches(cotangent.reshape(-1, width), micro)

    a_s = norm(source, gains[0], shifts[0])
    bias_s = (turned(shifts[3], cols), turned(shifts[4], cols))
    joined_s, weights_s, mixed_s, out_s = branch(
        a_s, pack_s, bias_s, cols, frame_shape, SPATIAL
    )
    h1 = (source + out_s + shifts[5]).astype(BF)
    h1 = to_patches(h1, micro).astype(F32)

    a_t = norm(h1, gains[1], shifts[1])
    bias_t = (turned(shifts[6], cols), turned(shifts[7], cols))
    joined_t, weights_t, mixed_t, out_t = branch(
        a_t, pack_t, bias_t, cols, clip_shape, TEMPORAL
    )
    h2 = h1 + out_t + shifts[8]
    a_m = norm(h2, gains[2], shifts[2])
    up_bias = turned(fc1, hidden)
    dyb = grad_out
    dy = grad_out.astype(F32)
    mixed = h2 + shifts[9]
    grad_am, sums_u, sums_d, sum_fc1 = 0.0, [], [], []
    for r in range(4):
        pre = dot(a_m, pack_u[r], ((1,), (0,))) + up_bias[r * hidden : (r + 1) * hidden]
        half = 0.5 * (1.0 + lax.erf(pre * 0.5**0.5))
        act = (pre * half).astype(BF)
        slope = half + pre * jnp.exp(-0.5 * pre * pre) * 0.3989422804014327
        mixed = mixed + dot(act, pack_d[r], ((1,), (1,)))
        grad_act = dot(dyb, pack_d[r], ((1,), (0,)))
        grad_pre = (grad_act * slope).astype(BF)
        sums_d.append(dot(dyb, act, ((0,), (0,))).astype(BF))
        sums_u.append(dot(a_m, grad_pre, ((0,), (0,))).astype(BF))
        sum_fc1.append(jnp.sum(grad_pre.astype(F32), axis=0))
        grad_am = grad_am + dot(grad_pre, pack_u[r], ((1,), (1,)))
    mixed = to_frames(mixed.astype(BF), micro)
    grad_d = reduce_all(sums_d)
    grad_u = reduce_all(sums_u)

    back, gain_m, shift_m = norm_back(h2, gains[2], grad_am)
    dh2 = dy + back
    grad_at, sums_t, bias_sums_t = branch_back(
        a_t, pack_t, (joined_t, weights_t, mixed_t), dh2.astype(BF), cols, clip_shape, TEMPORAL
    )
    grad_t = reduce_all(sums_t)
    back, gain_t, shift_t = norm_back(h1, gains[1], grad_at)
    dh1 = dh2 + back
    sum_dh1 = jnp.sum(dh1, axis=0)
    dh1 = to_frames(dh1.astype(BF), micro)
    grad_as, sums_s, bias_sums_s = branch_back(
        a_s, pack_s, (joined_s, weights_s, mixed_s), dh1, cols, frame_shape, SPATIAL
    )
    grad_s = reduce_all(sums_s)
    back, gain_s, shift_s = norm_back(source, gains[0], grad_as)
    grad_tokens = dh1.astype(F32) + back

    def placed(items, size):
        whole = jnp.zeros((4 * size,), F32)
        for r in range(4):
            whole = lax.dynamic_update_slice(whole, items[r], (order[r] * size,))
        return whole

    def split(vector, size):
        return [vector[r * size : (r + 1) * size] for r in range(4)]

    rows = [gain_s, gain_t, gain_m, shift_s, shift_t, shift_m]
    rows += [placed(split(item, cols), cols) for item in bias_sums_s]
    rows += [sum_dh1]
    rows += [placed(split(item, cols), cols) for item in bias_sums_t]
    rows += [jnp.sum(dh2, axis=0), jnp.sum(dy, axis=0)]
    table = jnp.stack(rows).reshape(13, wide_count, slim).swapaxes(0, 1)
    table = jnp.concatenate(
        [table, placed(sum_fc1, hidden).reshape(wide_count, extra - 13, slim)], axis=1
    )
    table = jnp.pad(table, ((0, 0), (0, -extra % 8), (0, 0)))
    height = table.shape[1]
    table = table.reshape(wide_count * height, slim)
    table = table + swap(table, "tensor", 1)
    table = table + swap(table, "tensor", 2)
    table = reduce_wide(table, F32)

    def unpack(total):
        w_qkv = jnp.stack([total[:, i * cols : (i + 1) * cols] for i in range(3)])
        return w_qkv, total[:, 3 * cols :].T

    qkv_s, out_s = unpack(grad_s)
    qkv_t, out_t = unpack(grad_t)
    return (
        mixed.reshape(tokens.shape),
        grad_tokens.reshape(tokens.shape),
        table[:3],
        table[3:13],
        table[13:extra].reshape(-1),
        qkv_s,
        out_s,
        qkv_t,
        out_t,
        grad_u,
        grad_d.T,
    )


def solution(mesh):
    specs = (
        P(None, ("wide", "tensor"), None),
        P(None, ("wide", "tensor"), None),
        P(None, "wide"),
        P(None, "wide"),
        P("wide"),
        P(None, "wide", "tensor"),
        P("tensor", "wide"),
        P(None, "wide", "tensor"),
        P("tensor", "wide"),
        P("wide", "tensor"),
        P("tensor", "wide"),
    )
    return jax.shard_map(
        per_device, mesh=mesh, in_specs=specs, out_specs=specs, check_vma=False
    )
```

```python
import jax
import jax.numpy as jnp
from jax import lax
from jax.experimental import pallas as pl
from jax.experimental.pallas import tpu as pltpu
from jax.sharding import PartitionSpec as P


HEAD_DIM = 64
PATCHES = 196
FRAMES = 16
FRAME_RUN = 2
EPSILON = 1e-06
RUNS = FRAMES // FRAME_RUN

BF = jnp.bfloat16
F32 = jnp.float32

SCALE = HEAD_DIM**-0.5
GROUP = 8
VMEM = pltpu.VMEM
LIMIT = 62 * 1024 * 1024


def cost(time_us):
    return pl.CostEstimate(flops=int(time_us * 1e9), bytes_accessed=0, transcendentals=0)


def norm_parts(rows):
    center = rows - jnp.mean(rows, axis=-1, keepdims=True)
    scale = lax.rsqrt(jnp.mean(center * center, axis=-1, keepdims=True) + EPSILON)
    return center * scale, scale


def norm(rows, gain, shift):
    hat, _ = norm_parts(rows)
    return (hat * gain + shift).astype(BF)


def norm_back(rows, gain, grad):
    hat, scale = norm_parts(rows)
    back = grad * gain
    inner = jnp.mean(back * hat, axis=-1, keepdims=True)
    result = scale * (back - jnp.mean(back, axis=-1, keepdims=True) - hat * inner)
    gain_sum = jnp.sum(grad * hat, axis=0, keepdims=True)
    return result, gain_sum, jnp.sum(grad, axis=0, keepdims=True)


def dot(left, right, dims=((1,), (0,))):
    return lax.dot_general(left, right, (dims, ((), ())), preferred_element_type=F32)


NT = ((1,), (1,))
TN = ((0,), (0,))


def softmax(scores, mask):
    if mask is not None:
        scores = jnp.where(mask, scores, -1e30)
    powers = jnp.exp(scores - jnp.max(scores, axis=-1, keepdims=True))
    return powers / jnp.sum(powers, axis=-1, keepdims=True)


def head_slices(head, cols):
    return [slice(which * cols + head * HEAD_DIM, which * cols + (head + 1) * HEAD_DIM) for which in range(4)]


def attend(block, cols, mask):
    results = []
    for head in range(cols // HEAD_DIM):
        q_at, k_at, v_at, _ = head_slices(head, cols)
        scores = dot(block[:, q_at], block[:, k_at], NT) * SCALE
        weights = softmax(scores, mask).astype(BF)
        results.append(dot(weights, block[:, v_at]).astype(BF))
    return results


def attend_back(block, grad_out, cols, mask, store):
    for head in range(cols // HEAD_DIM):
        q_at, k_at, v_at, _ = head_slices(head, cols)
        queries, key_rows, value_rows = block[:, q_at], block[:, k_at], block[:, v_at]
        grad = grad_out[:, head * HEAD_DIM : (head + 1) * HEAD_DIM]
        weights = softmax(dot(queries, key_rows, NT) * SCALE, mask)
        grad_w = dot(grad, value_rows, NT)
        inner = jnp.sum(weights * grad_w, axis=-1, keepdims=True)
        grad_s = (weights * (grad_w - inner)).astype(BF)
        store(q_at, (dot(grad_s, key_rows) * SCALE).astype(BF))
        store(k_at, (dot(grad_s, queries, TN) * SCALE).astype(BF))
        store(v_at, dot(weights.astype(BF), grad, TN).astype(BF))


def only_out(block, cut, skip):
    last = block[:, cut:]
    place = lax.broadcasted_iota(jnp.int32, last.shape, 1)
    return jnp.where(place < skip, jnp.zeros_like(last), last)


def fetch(sources, target, sem):
    copies = [
        pltpu.make_async_copy(item, target.at[r], sem.at[r]) for r, item in enumerate(sources)
    ]
    for copy in copies:
        copy.start()
    for copy in copies:
        copy.wait()


def cut_of(cols):
    cut = 3 * cols // 256 * 256
    return cut, 3 * cols - cut


def spatial_forward(rows, vecs, bias, packs, micro, share):
    frames, patches, width = rows.shape
    full = packs[0].shape[1]
    cols = full // 4
    cut, skip = cut_of(cols)
    padded = -(-share // GROUP) * GROUP
    pieces = patches // share

    def kernel(tok, vec, bia, w0, w1, w2, w3, a_out, x_out, h_out, wbuf, acc, sem):
        @pl.when(pl.program_id(0) == 0)
        def _():
            fetch((w0, w1, w2, w3), wbuf, sem)

        source = tok[0].astype(F32)
        normed = norm(source, vec[0:1], vec[1:2])
        a_out[0] = normed
        acc[...] = source + vec[2:3]

        def body(r, carry):
            x_out[0, r] = (dot(normed, wbuf[r]) + bia[r]).astype(BF)
            heads = attend(x_out[0, r], cols, None)
            for head, item in enumerate(heads):
                x_out[0, r, :, head_slices(head, cols)[3]] = item
            acc[...] += dot(only_out(x_out[0, r], cut, skip), wbuf[r, :, cut:], NT)
            return carry

        lax.fori_loop(0, 4, body, 0)
        h_out[...] = jnp.zeros_like(h_out)
        for piece in range(pieces):
            h_out[0, piece, 0, :share] = acc[piece * share : (piece + 1) * share].astype(BF)

    whole = pl.BlockSpec(memory_space=pl.ANY)
    return pl.pallas_call(
        kernel,
        name="spatial_forward",
        grid=(frames,),
        in_specs=[
            pl.BlockSpec((1, patches, width), lambda i: (i, 0, 0)),
            pl.BlockSpec(vecs.shape, lambda i: (0, 0)),
            pl.BlockSpec(bias.shape, lambda i: (0, 0, 0)),
            whole,
            whole,
            whole,
            whole,
        ],
        out_specs=[
            pl.BlockSpec((1, patches, width), lambda i: (i, 0, 0)),
            pl.BlockSpec((1, 4, patches, full), lambda i: (i, 0, 0, 0)),
            pl.BlockSpec(
                (1, pieces, 1, padded, width),
                lambda i: (i // FRAME_RUN, 0, i % FRAME_RUN, 0, 0),
            ),
        ],
        out_shape=[
            jax.ShapeDtypeStruct((frames, patches, width), BF),
            jax.ShapeDtypeStruct((frames, 4, patches, full), BF),
            jax.ShapeDtypeStruct((micro, pieces, FRAME_RUN, padded, width), BF),
        ],
        scratch_shapes=[
            VMEM((4, width, full), BF),
            VMEM((patches, width), F32),
            pltpu.SemaphoreType.DMA((4,)),
        ],
        cost_estimate=cost(30),
        compiler_params=pltpu.CompilerParams(vmem_limit_bytes=LIMIT),
    )(rows, vecs, bias, *packs)


def spatial_backward(rows, normed, kept, grad, vecs, packs, share):
    frames, patches, width = rows.shape
    full = packs[0].shape[1]
    cols = full // 4
    cut, skip = cut_of(cols)
    _, pieces, _, padded, _ = grad.shape

    def kernel(tok, nrm, x_in, g_in, vec, w0, w1, w2, w3, t_out, s_out, sums, b_out, wbuf, side, gbuf, acc, tot, sem):
        step = pl.program_id(0)

        @pl.when(step == 0)
        def _():
            fetch((w0, w1, w2, w3), wbuf, sem)
            tot[...] = jnp.zeros_like(tot)
            sums[...] = jnp.zeros_like(sums)
            b_out[...] = jnp.zeros_like(b_out)
            side[...] = jnp.zeros_like(side)

        for piece in range(pieces):
            gbuf[piece * share : (piece + 1) * share] = g_in[0, piece, 0, :share].astype(F32)
        grad_b = gbuf[...].astype(BF)
        acc[...] = jnp.zeros_like(acc)

        def body(r, carry):
            grad_o = dot(grad_b, wbuf[r, :, cut:])[:, skip:].astype(BF)

            def store(at, value):
                side[:, at] = value

            attend_back(x_in[0, r], grad_o, cols, None, store)
            acc[...] += dot(side[...], wbuf[r], NT)
            b_out[r] += jnp.sum(side[...].astype(F32), axis=0, keepdims=True)
            tot[r] += dot(nrm[0], side[...], TN)
            tot[r, :, cut:] += dot(grad_b, only_out(x_in[0, r], cut, skip), TN)
            return carry

        lax.fori_loop(0, 4, body, 0)
        back, gain_sum, shift_sum = norm_back(tok[0].astype(F32), vec[0:1], acc[...])
        t_out[0] = gbuf[...] + back
        sums[0:1] += gain_sum
        sums[1:2] += shift_sum

        @pl.when(step == frames - 1)
        def _():
            def last(r, carry):
                s_out[r] = tot[r].astype(BF)
                return carry

            lax.fori_loop(0, 4, last, 0)

    whole = pl.BlockSpec(memory_space=pl.ANY)
    frame = pl.BlockSpec((1, patches, width), lambda i: (i, 0, 0))
    return pl.pallas_call(
        kernel,
        name="spatial_backward",
        grid=(frames,),
        in_specs=[
            frame,
            frame,
            pl.BlockSpec((1, 4, patches, full), lambda i: (i, 0, 0, 0)),
            pl.BlockSpec(
                (1, pieces, 1, padded, width),
                lambda i: (i // FRAME_RUN, 0, i % FRAME_RUN, 0, 0),
            ),
            pl.BlockSpec(vecs.shape, lambda i: (0, 0)),
            whole,
            whole,
            whole,
            whole,
        ],
        out_specs=[
            frame,
            pl.BlockSpec((4, width, full), lambda i: (0, 0, 0)),
            pl.BlockSpec((8, width), lambda i: (0, 0)),
            pl.BlockSpec((4, 1, full), lambda i: (0, 0, 0)),
        ],
        out_shape=[
            jax.ShapeDtypeStruct((frames, patches, width), F32),
            jax.ShapeDtypeStruct((4, width, full), BF),
            jax.ShapeDtypeStruct((8, width), F32),
            jax.ShapeDtypeStruct((4, 1, full), F32),
        ],
        scratch_shapes=[
            VMEM((4, width, full), BF),
            VMEM((patches, full), BF),
            VMEM((patches, width), F32),
            VMEM((patches, width), F32),
            VMEM((4, width, full), F32),
            pltpu.SemaphoreType.DMA((4,)),
        ],
        cost_estimate=cost(50),
        compiler_params=pltpu.CompilerParams(vmem_limit_bytes=LIMIT),
    )(rows, normed, kept, grad, vecs, *packs)


def same_position(span):
    first = lax.broadcasted_iota(jnp.int32, (span, span), 0)
    second = lax.broadcasted_iota(jnp.int32, (span, span), 1)
    return first % GROUP == second % GROUP


def into_groups(source, target, groups):
    span = FRAMES * GROUP
    for at in range(groups):
        part = source[:, at * GROUP : (at + 1) * GROUP, :]
        target[at * span : (at + 1) * span] = part.reshape(span, part.shape[2])


def out_of_groups(source, stage, groups):
    span = FRAMES * GROUP
    for at in range(groups):
        part = source[at * span : (at + 1) * span]
        stage[:, at * GROUP : (at + 1) * GROUP, :] = part.reshape(FRAMES, GROUP, part.shape[1])


def whole_call(kernel, outs, scratch, *args):
    spaces = [pl.BlockSpec(memory_space=pltpu.VMEM if keep else pl.ANY) for keep, _ in args]
    return pl.pallas_call(
        kernel,
        in_specs=spaces,
        out_specs=[pl.BlockSpec(memory_space=pltpu.VMEM) for _ in outs],
        out_shape=[jax.ShapeDtypeStruct(shape, dtype) for shape, dtype in outs],
        scratch_shapes=scratch,
        cost_estimate=cost(45),
        compiler_params=pltpu.CompilerParams(vmem_limit_bytes=LIMIT),
    )(*[item for _, item in args])


def temporal_forward(block, vecs, bias, packs):
    frames, padded, width = block.shape
    full = packs[0].shape[1]
    cols = full // 4
    cut, skip = cut_of(cols)
    groups = padded // GROUP
    span = frames * GROUP
    rows = frames * padded

    def kernel(h_in, vec, bia, w0, w1, w2, w3, a_out, x_out, h_out, r_out, wbuf, stage, sem):
        fetch((w0, w1, w2, w3), wbuf, sem)
        stage[...] = h_in[...].astype(F32)
        into_groups(stage, h_out, groups)
        r_out[...] = h_out[...].astype(BF)
        a_out[...] = norm(h_out[...], vec[0:1], vec[1:2])
        h_out[...] += vec[2:3]
        mask = same_position(span)

        def body(r, carry):
            x_out[r] = (dot(a_out[...], wbuf[r]) + bia[r]).astype(BF)

            def inner(at, carry):
                here = pl.ds(pl.multiple_of(at * span, span), span)
                for head, item in enumerate(attend(x_out[r, here], cols, mask)):
                    x_out[r, here, head_slices(head, cols)[3]] = item
                return carry

            lax.fori_loop(0, groups, inner, 0)
            h_out[...] += dot(only_out(x_out[r], cut, skip), wbuf[r, :, cut:], NT)
            return carry

        lax.fori_loop(0, 4, body, 0)

    return whole_call(
        kernel,
        [((rows, width), BF), ((4, rows, full), BF), ((rows, width), F32), ((rows, width), BF)],
        [
            VMEM((4, width, full), BF),
            VMEM((frames, padded, width), F32),
            pltpu.SemaphoreType.DMA((4,)),
        ],
        (True, block),
        (True, vecs),
        (True, bias),
        *[(False, item) for item in packs],
    )


def feed_forward(h2, grad, vecs, up_bias, ups, downs):
    frames, padded, width = grad.shape
    rows = h2.shape[0]
    hidden = ups[0].shape[1]
    groups = padded // GROUP
    step = rows // 4

    def kernel(
        h_in, g_in, vec, bia, u0, u1, u2, u3, d0, d1, d2, d3,
        m_out, r_out, su_out, sd_out, sums, f_out,
        ubuf, dbuf, stage, dyb, am, act, pre, mix, dam, usem, dsem,
    ):
        fetch((u0, u1, u2, u3), ubuf, usem)
        fetch((d0, d1, d2, d3), dbuf, dsem)
        stage[...] = g_in[...].astype(F32)
        into_groups(stage, r_out, groups)
        dyb[...] = r_out[...].astype(BF)
        sums[...] = jnp.zeros_like(sums)
        sums[3:4] = jnp.sum(r_out[...], axis=0, keepdims=True)
        am[...] = norm(h_in[...], vec[0:1], vec[1:2])
        mix[...] = h_in[...] + vec[2:3]
        dam[...] = jnp.zeros_like(dam)

        def body(r, carry):
            def inner(at, total):
                here = pl.ds(pl.multiple_of(at * step, step), step)
                value = dot(am[here], ubuf[r]) + bia[r]
                half = 0.5 * (1.0 + lax.erf(value * 0.5**0.5))
                gate = (value * half).astype(BF)
                slope = half + value * jnp.exp(-0.5 * value * value) * 0.3989422804014327
                act[here] = gate
                mix[here] += dot(gate, dbuf[r], NT)
                grad_pre = (dot(dyb[here], dbuf[r]) * slope).astype(BF)
                pre[here] = grad_pre
                dam[here] += dot(grad_pre, ubuf[r], NT)
                return total + jnp.sum(grad_pre.astype(F32), axis=0, keepdims=True)

            f_out[r] = lax.fori_loop(0, 4, inner, jnp.zeros((1, hidden), F32))
            sd_out[r] = dot(dyb[...], act[...], TN).astype(BF)
            su_out[r] = dot(am[...], pre[...], TN).astype(BF)
            return carry

        lax.fori_loop(0, 4, body, 0)
        out_of_groups(mix, stage, groups)
        m_out[...] = stage[...].astype(BF)
        back, gain_sum, shift_sum = norm_back(h_in[...], vec[0:1], dam[...])
        r_out[...] += back
        sums[0:1] = gain_sum
        sums[1:2] = shift_sum
        sums[2:3] = jnp.sum(r_out[...], axis=0, keepdims=True)

    return whole_call(
        kernel,
        [
            ((frames, padded, width), BF),
            ((rows, width), F32),
            ((4, width, hidden), BF),
            ((4, width, hidden), BF),
            ((8, width), F32),
            ((4, 1, hidden), F32),
        ],
        [
            VMEM((4, width, hidden), BF),
            VMEM((4, width, hidden), BF),
            VMEM((frames, padded, width), F32),
            VMEM((rows, width), BF),
            VMEM((rows, width), BF),
            VMEM((rows, hidden), BF),
            VMEM((rows, hidden), BF),
            VMEM((rows, width), F32),
            VMEM((rows, width), F32),
            pltpu.SemaphoreType.DMA((4,)),
            pltpu.SemaphoreType.DMA((4,)),
        ],
        (True, h2),
        (True, grad),
        (True, vecs),
        (True, up_bias),
        *[(False, item) for item in ups],
        *[(False, item) for item in downs],
    )


def temporal_backward(grad, h1, normed, kept, vecs, packs, padded):
    rows, width = grad.shape
    full = packs[0].shape[1]
    cols = full // 4
    cut, skip = cut_of(cols)
    groups = padded // GROUP
    span = FRAMES * GROUP

    def kernel(g_in, h_in, nrm, x_in, vec, w0, w1, w2, w3, t_out, s_out, sums, b_out, wbuf, side, grad_b, grad_o, acc, stage, sem):
        fetch((w0, w1, w2, w3), wbuf, sem)
        grad_b[...] = g_in[...].astype(BF)
        acc[...] = jnp.zeros_like(acc)
        side[...] = jnp.zeros_like(side)
        sums[...] = jnp.zeros_like(sums)
        mask = same_position(span)

        def body(r, carry):
            grad_o[...] = dot(grad_b[...], wbuf[r, :, cut:]).astype(BF)

            def inner(at, carry):
                here = pl.ds(pl.multiple_of(at * span, span), span)

                def store(cols_at, value):
                    side[here, cols_at] = value

                attend_back(x_in[r, here], grad_o[here][:, skip:], cols, mask, store)
                return carry

            lax.fori_loop(0, groups, inner, 0)
            acc[...] += dot(side[...], wbuf[r], NT)
            b_out[r] = jnp.sum(side[...].astype(F32), axis=0, keepdims=True)
            first = dot(nrm[...], side[...], TN)
            second = dot(grad_b[...], only_out(x_in[r], cut, skip), TN)
            s_out[r, :, :cut] = first[:, :cut].astype(BF)
            s_out[r, :, cut:] = (first[:, cut:] + second).astype(BF)
            return carry

        lax.fori_loop(0, 4, body, 0)
        back, gain_sum, shift_sum = norm_back(h_in[...].astype(F32), vec[0:1], acc[...])
        acc[...] = g_in[...] + back
        sums[0:1] = gain_sum
        sums[1:2] = shift_sum
        sums[2:3] = jnp.sum(acc[...], axis=0, keepdims=True)
        out_of_groups(acc, stage, groups)
        t_out[...] = stage[...].astype(BF)

    return whole_call(
        kernel,
        [
            ((FRAMES, padded, width), BF),
            ((4, width, full), BF),
            ((8, width), F32),
            ((4, 1, full), F32),
        ],
        [
            VMEM((4, width, full), BF),
            VMEM((rows, full), BF),
            VMEM((rows, width), BF),
            VMEM((rows, full - cut), BF),
            VMEM((rows, width), F32),
            VMEM((FRAMES, padded, width), F32),
            pltpu.SemaphoreType.DMA((4,)),
        ],
        (True, grad),
        (True, h1),
        (True, normed),
        (True, kept),
        (True, vecs),
        *[(False, item) for item in packs],
    )


def assemble(pieces, me, rows):
    count = len(pieces)
    width = pieces[0].shape[1]
    rest = pieces[0].shape[0] - rows

    def kernel(me_ref, *refs):
        ins, outs = refs[:count], refs[count:]
        for bits in range(count):
            at = me_ref[0] ^ bits
            outs[0][pl.ds(pl.multiple_of(at * rows, rows), rows)] = ins[bits][:rows]
            if rest:
                outs[1][at] = ins[bits][rows:]

    shapes = [jax.ShapeDtypeStruct((count * rows, width), pieces[0].dtype)]
    if rest:
        shapes.append(jax.ShapeDtypeStruct((count, rest, width), pieces[0].dtype))
    spec = pl.BlockSpec(memory_space=pltpu.VMEM)
    return pl.pallas_call(
        kernel,
        name="assemble",
        in_specs=[pl.BlockSpec(memory_space=pltpu.SMEM)] + [spec] * count,
        out_specs=[spec] * len(shapes),
        out_shape=shapes,
    )(me.reshape(1), *pieces)


def swap(block, axis, bits):
    size = lax.axis_size(axis)
    return lax.ppermute(block, axis, [(i, i ^ bits) for i in range(size)])


def gather_wide(shard, rows):
    count = lax.axis_size("wide")
    if count != 8:
        whole = lax.all_gather(shard, "wide", axis=0)
        return whole[:, :rows].reshape(count * rows, -1), whole[:, rows:]
    pieces = {0: shard, 1: swap(shard, "wide", 1)}
    for bits in (6, 4, 2):
        pieces[bits] = swap(shard, "wide", bits)
    for bits in (6, 4, 2):
        pieces[bits ^ 1] = swap(pieces[bits], "wide", 1)
    result = assemble([pieces[bits] for bits in range(count)], lax.axis_index("wide"), rows)
    return result[0], result[1] if len(result) > 1 else None


def gather_tensor(block):
    far = swap(block, "tensor", 2)
    near = swap(block, "tensor", 1)
    return [block, near, far, swap(far, "tensor", 1)]


def reduce_all(parts):
    near = parts[0].astype(F32) + swap(parts[1], "tensor", 1).astype(F32)
    far = parts[2].astype(F32) + swap(parts[3], "tensor", 1).astype(F32)
    total = near + swap(far.astype(BF), "tensor", 2).astype(F32)
    return reduce_wide(total, BF)


def reduce_wide(total, link):
    count = lax.axis_size("wide")
    if count != 8:
        return lax.psum_scatter(total, "wide", scatter_dimension=0, tiled=True)
    me = lax.axis_index("wide")
    grid = total.reshape(4, 2, total.shape[0] // 8, total.shape[1])
    mine = lax.dynamic_index_in_dim(grid, me & 1, 1, keepdims=False)
    other = lax.dynamic_index_in_dim(grid, 1 - (me & 1), 1, keepdims=False)
    half = mine + swap(other.astype(link), "wide", 1).astype(F32)
    place = me >> 1
    result = lax.dynamic_index_in_dim(half, place, 0, keepdims=False)
    for bits in (1, 2, 3):
        piece = lax.dynamic_index_in_dim(half, place ^ bits, 0, keepdims=False)
        result = result + swap(piece.astype(link), "wide", bits * 2).astype(F32)
    return result


def exchange(block):
    count = lax.axis_size("wide")
    stride = count // RUNS
    groups = [[run * stride + clip for run in range(RUNS)] for clip in range(stride)]
    return lax.all_to_all(
        block, "wide", split_axis=0, concat_axis=0, tiled=True, axis_index_groups=groups
    )


def layer(
    tokens, cotangent, ln_gain, biases, fc1_bias, w_qkv_s, w_out_s, w_qkv_t, w_out_t, w_up, w_down
):
    micro, row_count, width = tokens.shape
    wide_count = lax.axis_size("wide")
    me_t = lax.axis_index("tensor")
    cols = w_qkv_s.shape[2]
    hidden = w_up.shape[1]
    slim = ln_gain.shape[1]
    share = micro * PATCHES // RUNS
    cut = PATCHES // share
    padded = -(-share // GROUP) * GROUP
    assert row_count == FRAME_RUN * PATCHES and lax.axis_size("tensor") == 4
    assert wide_count % RUNS == 0 and share * cut == PATCHES

    def pack(w_qkv, w_out):
        return jnp.concatenate([w_qkv[0], w_qkv[1], w_qkv[2], w_out.T], axis=1)

    small = jnp.concatenate([ln_gain, biases, fc1_bias.reshape(-1, slim)], axis=0)
    extra = small.shape[0]
    below = -(-small.size // (8 * 4 * cols)) * 8
    small = jnp.pad(small.reshape(-1), (0, below * 4 * cols - small.size))
    first = jnp.concatenate([pack(w_qkv_s, w_out_s), small.reshape(below, 4 * cols)], axis=0)
    whole_s, small = gather_wide(first, w_qkv_s.shape[1])
    pack_s = gather_tensor(whole_s)
    pack_t, pack_u, pack_d = [
        gather_tensor(gather_wide(shard, shard.shape[0])[0])
        for shard in (pack(w_qkv_t, w_out_t), w_up, w_down.T)
    ]

    small = small.reshape(wide_count, -1)[:, : extra * slim]
    small = small.reshape(wide_count, extra, slim).astype(F32)
    vectors = small[:, :13].swapaxes(0, 1).reshape(13, width)
    perm = me_t ^ jnp.arange(4)
    up_bias = small[:, 13:].reshape(4, 1, hidden)[perm]
    cut_cols = jnp.concatenate([vectors[6:8], vectors[9:11]]).reshape(4, 4, cols)[:, perm]
    gap = jnp.zeros((4, cols), F32)
    bias_s, bias_t = [
        jnp.concatenate([cut_cols[i], gap, cut_cols[i + 1], gap], axis=1)[:, None]
        for i in (0, 2)
    ]

    def vecs(*rows):
        return jnp.stack([vectors[i] for i in rows])

    frames = tokens.reshape(micro * FRAME_RUN, PATCHES, width)
    dy = cotangent.reshape(micro, FRAME_RUN, cut, share, width).swapaxes(1, 2)
    dy = jnp.pad(dy, ((0, 0), (0, 0), (0, 0), (0, padded - share), (0, 0)))
    dy = exchange(dy.reshape(RUNS, FRAME_RUN, padded, width)).reshape(FRAMES, padded, width)

    a_s, kept_s, h1 = spatial_forward(frames, vecs(0, 3, 8), bias_s, pack_s, micro, share)
    h1 = exchange(h1.reshape(RUNS, FRAME_RUN, padded, width)).reshape(FRAMES, padded, width)
    a_t, kept_t, h2, h1 = temporal_forward(h1, vecs(1, 4, 11), bias_t, pack_t)
    mixed, dh2, part_u, part_d, sums_m, sum_fc1 = feed_forward(
        h2, dy, vecs(2, 5, 12), up_bias, pack_u, pack_d
    )
    mixed = exchange(mixed.reshape(RUNS, FRAME_RUN, padded, width))
    mixed = mixed.reshape(micro, cut, FRAME_RUN, padded, width)[:, :, :, :share].swapaxes(1, 2)
    grad_d = reduce_all(part_d)
    grad_u = reduce_all(part_u)
    dh1, part_t, sums_t, side_t = temporal_backward(
        dh2, h1, a_t, kept_t, vecs(1, 4), pack_t, padded
    )
    dh1 = exchange(dh1.reshape(RUNS, FRAME_RUN, padded, width))
    dh1 = dh1.reshape(micro, cut, FRAME_RUN, padded, width)
    grad_t = reduce_all(part_t)
    grad_tokens, part_s, sums_s, side_s = spatial_backward(
        frames, a_s, kept_s, dh1, vecs(0, 3), pack_s, share
    )
    grad_s = reduce_all(part_s)

    sides = jnp.stack([side_s, side_t]).reshape(2, 4, 4, cols)[:, perm]
    sides = sides.swapaxes(1, 2).reshape(2, 4, width)
    rows = [sums_s[0:1], sums_t[0:1], sums_m[0:1], sums_s[1:2], sums_t[1:2], sums_m[1:2]]
    rows += [sides[0, 0:1], sides[0, 2:3], sums_t[2:3], sides[1, 0:1], sides[1, 2:3]]
    rows += [sums_m[2:3], sums_m[3:4]]
    table = jnp.concatenate(rows).reshape(13, wide_count, slim).swapaxes(0, 1)
    fc1 = sum_fc1[:, 0][perm].reshape(wide_count, extra - 13, slim)
    table = jnp.concatenate(
        [table, fc1, jnp.zeros((wide_count, -extra % 8, slim), F32)], axis=1
    )
    table = table.reshape(-1, slim)
    table = table + swap(table, "tensor", 1)
    table = table + swap(table, "tensor", 2)
    table = reduce_wide(table, F32)

    def unpack(total):
        w_qkv = jnp.stack([total[:, i * cols : (i + 1) * cols] for i in range(3)])
        return w_qkv, total[:, 3 * cols :].T

    qkv_s, out_s = unpack(grad_s)
    qkv_t, out_t = unpack(grad_t)
    return (
        mixed.reshape(tokens.shape),
        grad_tokens.reshape(tokens.shape),
        table[:3],
        table[3:13],
        table[13:extra].reshape(-1),
        qkv_s,
        out_s,
        qkv_t,
        out_t,
        grad_u,
        grad_d.T,
    )


def solution(mesh):
    specs = (
        P(None, ("wide", "tensor"), None),
        P(None, ("wide", "tensor"), None),
        P(None, "wide"),
        P(None, "wide"),
        P("wide"),
        P(None, "wide", "tensor"),
        P("tensor", "wide"),
        P(None, "wide", "tensor"),
        P("tensor", "wide"),
        P("wide", "tensor"),
        P("tensor", "wide"),
    )
    return jax.shard_map(layer, mesh=mesh, in_specs=specs, out_specs=specs, check_vma=False)
```

```python
import jax
import jax.numpy as jnp
from jax import lax
from jax.experimental import pallas as pl
from jax.experimental.pallas import tpu as pltpu
from jax.sharding import PartitionSpec as P


HEAD_DIM = 64
PATCHES = 196
FRAMES = 16
FRAME_RUN = 2
EPSILON = 1e-06
RUNS = FRAMES // FRAME_RUN

BF = jnp.bfloat16
F32 = jnp.float32

SCALE = HEAD_DIM**-0.5
GROUP = 8
VMEM = pltpu.VMEM
LIMIT = 62 * 1024 * 1024


def cost(time_us):
    return pl.CostEstimate(flops=int(time_us * 1e9), bytes_accessed=0, transcendentals=0)


def norm_parts(rows):
    center = rows - jnp.mean(rows, axis=-1, keepdims=True)
    scale = lax.rsqrt(jnp.mean(center * center, axis=-1, keepdims=True) + EPSILON)
    return center * scale, scale


def norm(rows, gain, shift):
    hat, _ = norm_parts(rows)
    return (hat * gain + shift).astype(BF)


def norm_back(rows, gain, grad):
    hat, scale = norm_parts(rows)
    back = grad * gain
    inner = jnp.mean(back * hat, axis=-1, keepdims=True)
    result = scale * (back - jnp.mean(back, axis=-1, keepdims=True) - hat * inner)
    gain_sum = jnp.sum(grad * hat, axis=0, keepdims=True)
    return result, gain_sum, jnp.sum(grad, axis=0, keepdims=True)


def dot(left, right, dims=((1,), (0,))):
    return lax.dot_general(left, right, (dims, ((), ())), preferred_element_type=F32)


NT = ((1,), (1,))
TN = ((0,), (0,))


def softmax(scores, mask):
    if mask is not None:
        scores = jnp.where(mask, scores, -1e30)
    powers = jnp.exp(scores - jnp.max(scores, axis=0, keepdims=True))
    return powers * (1.0 / jnp.sum(powers, axis=0, keepdims=True))


def head_slices(head, cols):
    return [slice(which * cols + head * HEAD_DIM, which * cols + (head + 1) * HEAD_DIM) for which in range(4)]


def attend(load, cols, spans, mask, scores, weights, store):
    units = [(span, *head_slices(head, cols)) for head in range(cols // HEAD_DIM) for span in spans]
    for at, (span, q_at, k_at, _, _) in enumerate(units):
        scores[at] = dot(load(span, k_at), load(span, q_at), NT)
    for at in range(len(units)):
        weights[at] = softmax(scores[at] * SCALE, mask).astype(BF)
    for at, (span, _, _, v_at, o_at) in enumerate(units):
        store(span, o_at, dot(weights[at], load(span, v_at), TN).astype(BF))


def attend_back(load, load_grad, cols, spans, mask, scores, grads, weights, turned, store):
    units = [
        (span, head, *head_slices(head, cols)) for head in range(cols // HEAD_DIM) for span in spans
    ]
    for at, (span, head, q_at, k_at, v_at, _) in enumerate(units):
        scores[at] = dot(load(span, k_at), load(span, q_at), NT)
        grads[at] = dot(load(span, v_at), load_grad(span, head), NT)
    for at in range(len(units)):
        soft = softmax(scores[at] * SCALE, mask)
        inner = jnp.sum(soft * grads[at], axis=0, keepdims=True)
        weights[at] = soft.astype(BF)
        turned[at] = (soft * (grads[at] - inner)).astype(BF)
    for at, (span, head, q_at, k_at, v_at, _) in enumerate(units):
        grad_s = turned[at]
        store(span, q_at, (dot(grad_s, load(span, k_at), TN) * SCALE).astype(BF))
        store(span, k_at, (dot(grad_s, load(span, q_at)) * SCALE).astype(BF))
        store(span, v_at, dot(weights[at], load_grad(span, head)).astype(BF))


def only_out(block, cut, skip):
    last = block[:, cut:]
    place = lax.broadcasted_iota(jnp.int32, last.shape, 1)
    return jnp.where(place < skip, jnp.zeros_like(last), last)


def fetch(sources, target, sem):
    copies = [
        pltpu.make_async_copy(item, target.at[r], sem.at[r]) for r, item in enumerate(sources)
    ]
    for copy in copies:
        copy.start()
    for copy in copies:
        copy.wait()


def cut_of(cols):
    cut = 3 * cols // 256 * 256
    return cut, 3 * cols - cut


def spatial_forward(rows, vecs, bias, packs, micro, share):
    frames, patches, width = rows.shape
    full = packs[0].shape[1]
    cols = full // 4
    cut, skip = cut_of(cols)
    padded = -(-share // GROUP) * GROUP
    pieces = patches // share

    def kernel(tok, vec, bia, w0, w1, w2, w3, a_out, x_out, h_out, wbuf, acc, sbuf, pbuf, sem):
        @pl.when(pl.program_id(0) == 0)
        def _():
            fetch((w0, w1, w2, w3), wbuf, sem)

        source = tok[0].astype(F32)
        normed = norm(source, vec[0:1], vec[1:2])
        a_out[0] = normed
        acc[...] = source + vec[2:3]

        def body(r, carry):
            x_out[0, r] = (dot(normed, wbuf[r]) + bia[r]).astype(BF)

            def load(span, at):
                return x_out[0, r, span, at]

            def store(span, at, value):
                x_out[0, r, span, at] = value

            attend(load, cols, [slice(0, patches)], None, sbuf, pbuf, store)
            acc[...] += dot(only_out(x_out[0, r], cut, skip), wbuf[r, :, cut:], NT)
            return carry

        lax.fori_loop(0, 4, body, 0)
        h_out[...] = jnp.zeros_like(h_out)
        for piece in range(pieces):
            h_out[0, piece, 0, :share] = acc[piece * share : (piece + 1) * share].astype(BF)

    whole = pl.BlockSpec(memory_space=pl.ANY)
    return pl.pallas_call(
        kernel,
        name="spatial_forward",
        grid=(frames,),
        in_specs=[
            pl.BlockSpec((1, patches, width), lambda i: (i, 0, 0)),
            pl.BlockSpec(vecs.shape, lambda i: (0, 0)),
            pl.BlockSpec(bias.shape, lambda i: (0, 0, 0)),
            whole,
            whole,
            whole,
            whole,
        ],
        out_specs=[
            pl.BlockSpec((1, patches, width), lambda i: (i, 0, 0)),
            pl.BlockSpec((1, 4, patches, full), lambda i: (i, 0, 0, 0)),
            pl.BlockSpec(
                (1, pieces, 1, padded, width),
                lambda i: (i // FRAME_RUN, 0, i % FRAME_RUN, 0, 0),
            ),
        ],
        out_shape=[
            jax.ShapeDtypeStruct((frames, patches, width), BF),
            jax.ShapeDtypeStruct((frames, 4, patches, full), BF),
            jax.ShapeDtypeStruct((micro, pieces, FRAME_RUN, padded, width), BF),
        ],
        scratch_shapes=[
            VMEM((4, width, full), BF),
            VMEM((patches, width), F32),
            VMEM((cols // HEAD_DIM, patches, patches), F32),
            VMEM((cols // HEAD_DIM, patches, patches), BF),
            pltpu.SemaphoreType.DMA((4,)),
        ],
        cost_estimate=cost(30),
        compiler_params=pltpu.CompilerParams(vmem_limit_bytes=LIMIT),
    )(rows, vecs, bias, *packs)


def spatial_backward(rows, normed, kept, grad, vecs, packs, share):
    frames, patches, width = rows.shape
    full = packs[0].shape[1]
    cols = full // 4
    cut, skip = cut_of(cols)
    _, pieces, _, padded, _ = grad.shape

    def kernel(tok, nrm, x_in, g_in, vec, w0, w1, w2, w3, t_out, s_out, sums, b_out, wbuf, side, gbuf, acc, tot, grad_o, sbuf, dbuf, pbuf, tbuf, sem):
        step = pl.program_id(0)

        @pl.when(step == 0)
        def _():
            fetch((w0, w1, w2, w3), wbuf, sem)
            tot[...] = jnp.zeros_like(tot)
            sums[...] = jnp.zeros_like(sums)
            b_out[...] = jnp.zeros_like(b_out)
            side[...] = jnp.zeros_like(side)

        for piece in range(pieces):
            gbuf[piece * share : (piece + 1) * share] = g_in[0, piece, 0, :share].astype(F32)
        grad_b = gbuf[...].astype(BF)
        acc[...] = jnp.zeros_like(acc)

        def body(r, carry):
            grad_o[...] = dot(grad_b, wbuf[r, :, cut:]).astype(BF)

            def load(span, at):
                return x_in[0, r, span, at]

            def load_grad(span, head):
                return grad_o[span, skip + head * HEAD_DIM : skip + (head + 1) * HEAD_DIM]

            def store(span, at, value):
                side[span, at] = value

            attend_back(
                load, load_grad, cols, [slice(0, patches)], None, sbuf, dbuf, pbuf, tbuf, store
            )
            acc[...] += dot(side[...], wbuf[r], NT)
            b_out[r] += jnp.sum(side[...].astype(F32), axis=0, keepdims=True)
            tot[r] += dot(nrm[0], side[...], TN)
            tot[r, :, cut:] += dot(grad_b, only_out(x_in[0, r], cut, skip), TN)
            return carry

        lax.fori_loop(0, 4, body, 0)
        back, gain_sum, shift_sum = norm_back(tok[0].astype(F32), vec[0:1], acc[...])
        t_out[0] = gbuf[...] + back
        sums[0:1] += gain_sum
        sums[1:2] += shift_sum

        @pl.when(step == frames - 1)
        def _():
            def last(r, carry):
                s_out[r] = tot[r].astype(BF)
                return carry

            lax.fori_loop(0, 4, last, 0)

    whole = pl.BlockSpec(memory_space=pl.ANY)
    frame = pl.BlockSpec((1, patches, width), lambda i: (i, 0, 0))
    return pl.pallas_call(
        kernel,
        name="spatial_backward",
        grid=(frames,),
        in_specs=[
            frame,
            frame,
            pl.BlockSpec((1, 4, patches, full), lambda i: (i, 0, 0, 0)),
            pl.BlockSpec(
                (1, pieces, 1, padded, width),
                lambda i: (i // FRAME_RUN, 0, i % FRAME_RUN, 0, 0),
            ),
            pl.BlockSpec(vecs.shape, lambda i: (0, 0)),
            whole,
            whole,
            whole,
            whole,
        ],
        out_specs=[
            frame,
            pl.BlockSpec((4, width, full), lambda i: (0, 0, 0)),
            pl.BlockSpec((8, width), lambda i: (0, 0)),
            pl.BlockSpec((4, 1, full), lambda i: (0, 0, 0)),
        ],
        out_shape=[
            jax.ShapeDtypeStruct((frames, patches, width), F32),
            jax.ShapeDtypeStruct((4, width, full), BF),
            jax.ShapeDtypeStruct((8, width), F32),
            jax.ShapeDtypeStruct((4, 1, full), F32),
        ],
        scratch_shapes=[
            VMEM((4, width, full), BF),
            VMEM((patches, full), BF),
            VMEM((patches, width), F32),
            VMEM((patches, width), F32),
            VMEM((4, width, full), F32),
            VMEM((patches, full - cut), BF),
            VMEM((cols // HEAD_DIM, patches, patches), F32),
            VMEM((cols // HEAD_DIM, patches, patches), F32),
            VMEM((cols // HEAD_DIM, patches, patches), BF),
            VMEM((cols // HEAD_DIM, patches, patches), BF),
            pltpu.SemaphoreType.DMA((4,)),
        ],
        cost_estimate=cost(50),
        compiler_params=pltpu.CompilerParams(vmem_limit_bytes=LIMIT),
    )(rows, normed, kept, grad, vecs, *packs)


def same_position(span):
    first = lax.broadcasted_iota(jnp.int32, (span, span), 0)
    second = lax.broadcasted_iota(jnp.int32, (span, span), 1)
    return first % GROUP == second % GROUP


def into_groups(source, target, groups):
    span = FRAMES * GROUP
    for at in range(groups):
        part = source[:, at * GROUP : (at + 1) * GROUP, :]
        target[at * span : (at + 1) * span] = part.reshape(span, part.shape[2])


def out_of_groups(source, stage, groups):
    span = FRAMES * GROUP
    for at in range(groups):
        part = source[at * span : (at + 1) * span]
        stage[:, at * GROUP : (at + 1) * GROUP, :] = part.reshape(FRAMES, GROUP, part.shape[1])


def whole_call(kernel, outs, scratch, *args):
    spaces = [pl.BlockSpec(memory_space=pltpu.VMEM if keep else pl.ANY) for keep, _ in args]
    return pl.pallas_call(
        kernel,
        in_specs=spaces,
        out_specs=[pl.BlockSpec(memory_space=pltpu.VMEM) for _ in outs],
        out_shape=[jax.ShapeDtypeStruct(shape, dtype) for shape, dtype in outs],
        scratch_shapes=scratch,
        cost_estimate=cost(45),
        compiler_params=pltpu.CompilerParams(vmem_limit_bytes=LIMIT),
    )(*[item for _, item in args])


def temporal_forward(block, vecs, bias, packs):
    frames, padded, width = block.shape
    full = packs[0].shape[1]
    cols = full // 4
    cut, skip = cut_of(cols)
    groups = padded // GROUP
    span = frames * GROUP
    rows = frames * padded
    spans = [slice(at * span, (at + 1) * span) for at in range(groups)]
    units = groups * cols // HEAD_DIM

    def kernel(h_in, vec, bia, w0, w1, w2, w3, a_out, x_out, h_out, r_out, wbuf, stage, sbuf, pbuf, sem):
        fetch((w0, w1, w2, w3), wbuf, sem)
        stage[...] = h_in[...].astype(F32)
        into_groups(stage, h_out, groups)
        r_out[...] = h_out[...].astype(BF)
        a_out[...] = norm(h_out[...], vec[0:1], vec[1:2])
        h_out[...] += vec[2:3]
        mask = same_position(span)

        def body(r, carry):
            x_out[r] = (dot(a_out[...], wbuf[r]) + bia[r]).astype(BF)

            def load(here, at):
                return x_out[r, here, at]

            def store(here, at, value):
                x_out[r, here, at] = value

            attend(load, cols, spans, mask, sbuf, pbuf, store)
            h_out[...] += dot(only_out(x_out[r], cut, skip), wbuf[r, :, cut:], NT)
            return carry

        lax.fori_loop(0, 4, body, 0)

    return whole_call(
        kernel,
        [((rows, width), BF), ((4, rows, full), BF), ((rows, width), F32), ((rows, width), BF)],
        [
            VMEM((4, width, full), BF),
            VMEM((frames, padded, width), F32),
            VMEM((units, span, span), F32),
            VMEM((units, span, span), BF),
            pltpu.SemaphoreType.DMA((4,)),
        ],
        (True, block),
        (True, vecs),
        (True, bias),
        *[(False, item) for item in packs],
    )


def feed_forward(h2, grad, vecs, up_bias, ups, downs):
    frames, padded, width = grad.shape
    rows = h2.shape[0]
    hidden = ups[0].shape[1]
    groups = padded // GROUP
    step = rows // 4

    def kernel(
        h_in, g_in, vec, bia, u0, u1, u2, u3, d0, d1, d2, d3,
        m_out, r_out, su_out, sd_out, sums, f_out,
        ubuf, dbuf, stage, dyb, am, act, pre, mix, dam, usem, dsem,
    ):
        fetch((u0, u1, u2, u3), ubuf, usem)
        fetch((d0, d1, d2, d3), dbuf, dsem)
        stage[...] = g_in[...].astype(F32)
        into_groups(stage, r_out, groups)
        dyb[...] = r_out[...].astype(BF)
        sums[...] = jnp.zeros_like(sums)
        sums[3:4] = jnp.sum(r_out[...], axis=0, keepdims=True)
        am[...] = norm(h_in[...], vec[0:1], vec[1:2])
        mix[...] = h_in[...] + vec[2:3]
        dam[...] = jnp.zeros_like(dam)

        def body(r, carry):
            def inner(at, total):
                here = pl.ds(pl.multiple_of(at * step, step), step)
                value = dot(am[here], ubuf[r]) + bia[r]
                half = 0.5 * (1.0 + lax.erf(value * 0.5**0.5))
                gate = (value * half).astype(BF)
                slope = half + value * jnp.exp(-0.5 * value * value) * 0.3989422804014327
                act[here] = gate
                mix[here] += dot(gate, dbuf[r], NT)
                grad_pre = (dot(dyb[here], dbuf[r]) * slope).astype(BF)
                pre[here] = grad_pre
                dam[here] += dot(grad_pre, ubuf[r], NT)
                return total + jnp.sum(grad_pre.astype(F32), axis=0, keepdims=True)

            f_out[r] = lax.fori_loop(0, 4, inner, jnp.zeros((1, hidden), F32))
            sd_out[r] = dot(dyb[...], act[...], TN).astype(BF)
            su_out[r] = dot(am[...], pre[...], TN).astype(BF)
            return carry

        lax.fori_loop(0, 4, body, 0)
        out_of_groups(mix, stage, groups)
        m_out[...] = stage[...].astype(BF)
        back, gain_sum, shift_sum = norm_back(h_in[...], vec[0:1], dam[...])
        r_out[...] += back
        sums[0:1] = gain_sum
        sums[1:2] = shift_sum
        sums[2:3] = jnp.sum(r_out[...], axis=0, keepdims=True)

    return whole_call(
        kernel,
        [
            ((frames, padded, width), BF),
            ((rows, width), F32),
            ((4, width, hidden), BF),
            ((4, width, hidden), BF),
            ((8, width), F32),
            ((4, 1, hidden), F32),
        ],
        [
            VMEM((4, width, hidden), BF),
            VMEM((4, width, hidden), BF),
            VMEM((frames, padded, width), F32),
            VMEM((rows, width), BF),
            VMEM((rows, width), BF),
            VMEM((rows, hidden), BF),
            VMEM((rows, hidden), BF),
            VMEM((rows, width), F32),
            VMEM((rows, width), F32),
            pltpu.SemaphoreType.DMA((4,)),
            pltpu.SemaphoreType.DMA((4,)),
        ],
        (True, h2),
        (True, grad),
        (True, vecs),
        (True, up_bias),
        *[(False, item) for item in ups],
        *[(False, item) for item in downs],
    )


def temporal_backward(grad, h1, normed, kept, vecs, packs, padded):
    rows, width = grad.shape
    full = packs[0].shape[1]
    cols = full // 4
    cut, skip = cut_of(cols)
    groups = padded // GROUP
    span = FRAMES * GROUP
    spans = [slice(at * span, (at + 1) * span) for at in range(groups)]
    units = groups * cols // HEAD_DIM

    def kernel(g_in, h_in, nrm, x_in, vec, w0, w1, w2, w3, t_out, s_out, sums, b_out, wbuf, side, grad_b, grad_o, acc, stage, sbuf, dbuf, pbuf, tbuf, sem):
        fetch((w0, w1, w2, w3), wbuf, sem)
        grad_b[...] = g_in[...].astype(BF)
        acc[...] = jnp.zeros_like(acc)
        side[...] = jnp.zeros_like(side)
        sums[...] = jnp.zeros_like(sums)
        mask = same_position(span)

        def body(r, carry):
            grad_o[...] = dot(grad_b[...], wbuf[r, :, cut:]).astype(BF)

            def load(here, at):
                return x_in[r, here, at]

            def load_grad(here, head):
                return grad_o[here, skip + head * HEAD_DIM : skip + (head + 1) * HEAD_DIM]

            def store(here, at, value):
                side[here, at] = value

            attend_back(load, load_grad, cols, spans, mask, sbuf, dbuf, pbuf, tbuf, store)
            acc[...] += dot(side[...], wbuf[r], NT)
            b_out[r] = jnp.sum(side[...].astype(F32), axis=0, keepdims=True)
            first = dot(nrm[...], side[...], TN)
            second = dot(grad_b[...], only_out(x_in[r], cut, skip), TN)
            s_out[r, :, :cut] = first[:, :cut].astype(BF)
            s_out[r, :, cut:] = (first[:, cut:] + second).astype(BF)
            return carry

        lax.fori_loop(0, 4, body, 0)
        back, gain_sum, shift_sum = norm_back(h_in[...].astype(F32), vec[0:1], acc[...])
        acc[...] = g_in[...] + back
        sums[0:1] = gain_sum
        sums[1:2] = shift_sum
        sums[2:3] = jnp.sum(acc[...], axis=0, keepdims=True)
        out_of_groups(acc, stage, groups)
        t_out[...] = stage[...].astype(BF)

    return whole_call(
        kernel,
        [
            ((FRAMES, padded, width), BF),
            ((4, width, full), BF),
            ((8, width), F32),
            ((4, 1, full), F32),
        ],
        [
            VMEM((4, width, full), BF),
            VMEM((rows, full), BF),
            VMEM((rows, width), BF),
            VMEM((rows, full - cut), BF),
            VMEM((rows, width), F32),
            VMEM((FRAMES, padded, width), F32),
            VMEM((units, span, span), F32),
            VMEM((units, span, span), F32),
            VMEM((units, span, span), BF),
            VMEM((units, span, span), BF),
            pltpu.SemaphoreType.DMA((4,)),
        ],
        (True, grad),
        (True, h1),
        (True, normed),
        (True, kept),
        (True, vecs),
        *[(False, item) for item in packs],
    )


def assemble(pieces, me, rows):
    count = len(pieces)
    width = pieces[0].shape[1]
    rest = pieces[0].shape[0] - rows

    def kernel(me_ref, *refs):
        ins, outs = refs[:count], refs[count:]
        for bits in range(count):
            at = me_ref[0] ^ bits
            outs[0][pl.ds(pl.multiple_of(at * rows, rows), rows)] = ins[bits][:rows]
            if rest:
                outs[1][at] = ins[bits][rows:]

    shapes = [jax.ShapeDtypeStruct((count * rows, width), pieces[0].dtype)]
    if rest:
        shapes.append(jax.ShapeDtypeStruct((count, rest, width), pieces[0].dtype))
    spec = pl.BlockSpec(memory_space=pltpu.VMEM)
    return pl.pallas_call(
        kernel,
        name="assemble",
        in_specs=[pl.BlockSpec(memory_space=pltpu.SMEM)] + [spec] * count,
        out_specs=[spec] * len(shapes),
        out_shape=shapes,
    )(me.reshape(1), *pieces)


def swap(block, axis, bits):
    size = lax.axis_size(axis)
    return lax.ppermute(block, axis, [(i, i ^ bits) for i in range(size)])


def gather_wide(shard, rows):
    count = lax.axis_size("wide")
    if count != 8:
        whole = lax.all_gather(shard, "wide", axis=0)
        return whole[:, :rows].reshape(count * rows, -1), whole[:, rows:]
    pieces = {0: shard, 1: swap(shard, "wide", 1)}
    for bits in (6, 4, 2):
        pieces[bits] = swap(shard, "wide", bits)
    for bits in (6, 4, 2):
        pieces[bits ^ 1] = swap(pieces[bits], "wide", 1)
    result = assemble([pieces[bits] for bits in range(count)], lax.axis_index("wide"), rows)
    return result[0], result[1] if len(result) > 1 else None


def gather_tensor(block):
    far = swap(block, "tensor", 2)
    near = swap(block, "tensor", 1)
    return [block, near, far, swap(far, "tensor", 1)]


def reduce_all(parts):
    near = parts[0].astype(F32) + swap(parts[1], "tensor", 1).astype(F32)
    far = parts[2].astype(F32) + swap(parts[3], "tensor", 1).astype(F32)
    total = near + swap(far.astype(BF), "tensor", 2).astype(F32)
    return reduce_wide(total, BF)


def reduce_wide(total, link):
    count = lax.axis_size("wide")
    if count != 8:
        return lax.psum_scatter(total, "wide", scatter_dimension=0, tiled=True)
    me = lax.axis_index("wide")
    grid = total.reshape(4, 2, total.shape[0] // 8, total.shape[1])
    mine = lax.dynamic_index_in_dim(grid, me & 1, 1, keepdims=False)
    other = lax.dynamic_index_in_dim(grid, 1 - (me & 1), 1, keepdims=False)
    half = mine + swap(other.astype(link), "wide", 1).astype(F32)
    place = me >> 1
    result = lax.dynamic_index_in_dim(half, place, 0, keepdims=False)
    for bits in (1, 2, 3):
        piece = lax.dynamic_index_in_dim(half, place ^ bits, 0, keepdims=False)
        result = result + swap(piece.astype(link), "wide", bits * 2).astype(F32)
    return result


def exchange(block):
    count = lax.axis_size("wide")
    stride = count // RUNS
    groups = [[run * stride + clip for run in range(RUNS)] for clip in range(stride)]
    return lax.all_to_all(
        block, "wide", split_axis=0, concat_axis=0, tiled=True, axis_index_groups=groups
    )


def layer(
    tokens, cotangent, ln_gain, biases, fc1_bias, w_qkv_s, w_out_s, w_qkv_t, w_out_t, w_up, w_down
):
    micro, row_count, width = tokens.shape
    wide_count = lax.axis_size("wide")
    me_t = lax.axis_index("tensor")
    cols = w_qkv_s.shape[2]
    hidden = w_up.shape[1]
    slim = ln_gain.shape[1]
    share = micro * PATCHES // RUNS
    cut = PATCHES // share
    padded = -(-share // GROUP) * GROUP
    assert row_count == FRAME_RUN * PATCHES and lax.axis_size("tensor") == 4
    assert wide_count % RUNS == 0 and share * cut == PATCHES

    def pack(w_qkv, w_out):
        return jnp.concatenate([w_qkv[0], w_qkv[1], w_qkv[2], w_out.T], axis=1)

    small = jnp.concatenate([ln_gain, biases, fc1_bias.reshape(-1, slim)], axis=0)
    extra = small.shape[0]
    below = -(-small.size // (8 * 4 * cols)) * 8
    small = jnp.pad(small.reshape(-1), (0, below * 4 * cols - small.size))
    first = jnp.concatenate([pack(w_qkv_s, w_out_s), small.reshape(below, 4 * cols)], axis=0)
    whole_s, small = gather_wide(first, w_qkv_s.shape[1])
    pack_s = gather_tensor(whole_s)
    pack_t, pack_u, pack_d = [
        gather_tensor(gather_wide(shard, shard.shape[0])[0])
        for shard in (pack(w_qkv_t, w_out_t), w_up, w_down.T)
    ]

    small = small.reshape(wide_count, -1)[:, : extra * slim]
    small = small.reshape(wide_count, extra, slim).astype(F32)
    vectors = small[:, :13].swapaxes(0, 1).reshape(13, width)
    perm = me_t ^ jnp.arange(4)
    up_bias = small[:, 13:].reshape(4, 1, hidden)[perm]
    cut_cols = jnp.concatenate([vectors[6:8], vectors[9:11]]).reshape(4, 4, cols)[:, perm]
    gap = jnp.zeros((4, cols), F32)
    bias_s, bias_t = [
        jnp.concatenate([cut_cols[i], gap, cut_cols[i + 1], gap], axis=1)[:, None]
        for i in (0, 2)
    ]

    def vecs(*rows):
        return jnp.stack([vectors[i] for i in rows])

    frames = tokens.reshape(micro * FRAME_RUN, PATCHES, width)
    dy = cotangent.reshape(micro, FRAME_RUN, cut, share, width).swapaxes(1, 2)
    dy = jnp.pad(dy, ((0, 0), (0, 0), (0, 0), (0, padded - share), (0, 0)))
    dy = exchange(dy.reshape(RUNS, FRAME_RUN, padded, width)).reshape(FRAMES, padded, width)

    a_s, kept_s, h1 = spatial_forward(frames, vecs(0, 3, 8), bias_s, pack_s, micro, share)
    h1 = exchange(h1.reshape(RUNS, FRAME_RUN, padded, width)).reshape(FRAMES, padded, width)
    a_t, kept_t, h2, h1 = temporal_forward(h1, vecs(1, 4, 11), bias_t, pack_t)
    mixed, dh2, part_u, part_d, sums_m, sum_fc1 = feed_forward(
        h2, dy, vecs(2, 5, 12), up_bias, pack_u, pack_d
    )
    grad_d = reduce_all(part_d)
    grad_u = reduce_all(part_u)
    dh1, part_t, sums_t, side_t = temporal_backward(
        dh2, h1, a_t, kept_t, vecs(1, 4), pack_t, padded
    )
    dh1 = exchange(dh1.reshape(RUNS, FRAME_RUN, padded, width))
    mixed, dh1 = lax.optimization_barrier((mixed, dh1))
    mixed = exchange(mixed.reshape(RUNS, FRAME_RUN, padded, width))
    mixed = mixed.reshape(micro, cut, FRAME_RUN, padded, width)[:, :, :, :share].swapaxes(1, 2)
    dh1 = dh1.reshape(micro, cut, FRAME_RUN, padded, width)
    grad_t = reduce_all(part_t)
    grad_tokens, part_s, sums_s, side_s = spatial_backward(
        frames, a_s, kept_s, dh1, vecs(0, 3), pack_s, share
    )
    grad_s = reduce_all(part_s)

    sides = jnp.stack([side_s, side_t]).reshape(2, 4, 4, cols)[:, perm]
    sides = sides.swapaxes(1, 2).reshape(2, 4, width)
    rows = [sums_s[0:1], sums_t[0:1], sums_m[0:1], sums_s[1:2], sums_t[1:2], sums_m[1:2]]
    rows += [sides[0, 0:1], sides[0, 2:3], sums_t[2:3], sides[1, 0:1], sides[1, 2:3]]
    rows += [sums_m[2:3], sums_m[3:4]]
    table = jnp.concatenate(rows).reshape(13, wide_count, slim).swapaxes(0, 1)
    fc1 = sum_fc1[:, 0][perm].reshape(wide_count, extra - 13, slim)
    table = jnp.concatenate(
        [table, fc1, jnp.zeros((wide_count, -extra % 8, slim), F32)], axis=1
    )
    table = table.reshape(-1, slim)
    table = table + swap(table, "tensor", 1)
    table = table + swap(table, "tensor", 2)
    table = reduce_wide(table, F32)

    def unpack(total):
        w_qkv = jnp.stack([total[:, i * cols : (i + 1) * cols] for i in range(3)])
        return w_qkv, total[:, 3 * cols :].T

    qkv_s, out_s = unpack(grad_s)
    qkv_t, out_t = unpack(grad_t)
    return (
        mixed.reshape(tokens.shape),
        grad_tokens.reshape(tokens.shape),
        table[:3],
        table[3:13],
        table[13:extra].reshape(-1),
        qkv_s,
        out_s,
        qkv_t,
        out_t,
        grad_u,
        grad_d.T,
    )


def solution(mesh):
    specs = (
        P(None, ("wide", "tensor"), None),
        P(None, ("wide", "tensor"), None),
        P(None, "wide"),
        P(None, "wide"),
        P("wide"),
        P(None, "wide", "tensor"),
        P("tensor", "wide"),
        P(None, "wide", "tensor"),
        P("tensor", "wide"),
        P("wide", "tensor"),
        P("tensor", "wide"),
    )
    return jax.shard_map(layer, mesh=mesh, in_specs=specs, out_specs=specs, check_vma=False)
```
